128 devices in a mesh: cfg: 2 (over core), req: 4 (over y), seq: 16 (over z, x).
Axes of the slice: x: 4, y: 4, z: 4, core: 2. Of those that a mesh axis runs over, the one named last changes fastest.
Arguments:
- latent: float32 [8, 2048, 64], P('req', 'seq'), may hold values from -6 to 6
- hidden_in: bfloat16 [2, 8, 2048, 2432], P('cfg', 'req', 'seq'), may hold values from -25 to 25
- img_query: bfloat16 [2, 8, 2048, 2432], P('cfg', 'req', 'seq'), may hold values from -10 to 10
- img_key: bfloat16 [2, 8, 2048, 2432], P('cfg', 'req', 'seq'), may hold values from -10 to 10
- img_value: bfloat16 [2, 8, 2048, 2432], P('cfg', 'req', 'seq'), may hold values from -6 to 6
- txt_key: bfloat16 [2, 8, 160, 2432], P('cfg', 'req', 'seq'), may hold values from -10 to 10
- txt_value: bfloat16 [2, 8, 160, 2432], P('cfg', 'req', 'seq'), may hold values from -6 to 6
- text_len: int32 [2, 8], P('cfg', 'req'), may hold values from 38 to 154, as said below
- head_slot: int32 [38], replicated, may hold values from 0 to 47, as said below
- out_weight: bfloat16 [2432, 2432], replicated, may hold values from -0.125 to 0.125
- out_bias: float32 [2432], replicated, may hold values from -3 to 3
- attn_gate: float32 [2, 8, 2432], P('cfg', 'req'), may hold values from 0.5 to 2
- final_mod: float32 [2, 8, 2, 2432], P('cfg', 'req'), may hold values from -3 to 3
- final_weight: bfloat16 [2432, 64], replicated, may hold values from -0.125 to 0.125
- final_bias: float32 [64], replicated, may hold values from -3 to 3
- timesteps: int32 [8], P('req'), may hold values from 1 to 28
- guidance: float32 [8], P('req'), may hold values from 2.5 to 6
Outputs:
- velocity: float32 [8, 2048, 64], P('req', 'seq')
- latent_next: float32 [8, 2048, 64], P('req', 'seq')
- hidden_norms: float32 [2, 8], P('cfg', 'req')
- max_logits: float32 [48], P('seq')
The draws below stay inside these ranges and needn't reach their ends.
Inputs may be any that keep to these rules, and one draw needn't show every extreme that they name: `head_slot`: distinct heads take distinct slots; slots j * 3 to (j + 1) * 3 - 1 belong to index j of seq, and every index holds 3 heads or one fewer. Text positions below text_len are live; some half and request has exactly 154 live text tokens.
All inputs are finite; a program needn't handle non-finite values.
Results may differ from the reference program's by a relative error of at most 0.0032.
Values may be sent and summed in bfloat16 or wider, within the bound.
No kernel may reach another device: no remote copies, remote signals or barrier semaphores. Data moves between devices by JAX's collectives and lax.ppermute only.
A program may use at most 128 MiB of HBM per device.

```python
import math
import jax
import jax.numpy as jnp
from jax import lax

HEADS = 38
HD = 64
D = 2432
C_OUT = 64
IMG = 2048
TXT_LIVE = 154
TXT = 160
REQS = 8
STEPS = 28
HSLOT = 3
SLOTS = 48
N_SEQ = 16


def base_noise(noise_key, shape):
    return jnp.clip(jax.random.normal(noise_key, shape), -4.0, 4.0)


def draw_img_query(key, part):
    own_key = jax.random.fold_in(key, 31)
    noise_key, scale_key = jax.random.split(own_key)
    head_scale = jnp.exp(jax.random.uniform(scale_key, (2, REQS, 1, HEADS, 1), minval=0.0, maxval=math.log(1.8)))
    query_draw = (base_noise(noise_key, (2, REQS, IMG, HEADS, HD)) * head_scale).reshape(2, REQS, IMG, D)
    return query_draw.astype(jnp.bfloat16)


def draw_img_key(key, part):
    own_key = jax.random.fold_in(key, 37)
    key_draw = 1.2 * base_noise(own_key, (2, REQS, IMG, D))
    return key_draw.astype(jnp.bfloat16)


def draw_txt_key(key, part):
    own_key = jax.random.fold_in(key, 41)
    return (1.5 * base_noise(own_key, (2, REQS, TXT, D))).astype(jnp.bfloat16)


def draw_hidden_in(key, part):
    own_key = jax.random.fold_in(key, 43)
    noise_key, column_key = jax.random.split(own_key, 2)
    fraction = (jnp.arange(IMG, dtype=jnp.float32) / (IMG - 1))[None, None, :, None]
    column = jnp.exp(jax.random.uniform(column_key, (1, 1, 1, D), minval=0.0, maxval=math.log(10.0)))
    noise = jnp.clip(jax.random.normal(noise_key, (2, REQS, IMG, D)), -4.0, 4.0)
    result = 0.1 * noise * jnp.power(3.0, fraction) * column
    return result.astype(jnp.bfloat16)


def draw_text_len(key, part):
    own_key = jax.random.fold_in(key, 13)
    len_key, pick_key = jax.random.split(own_key)
    lengths = jax.random.randint(len_key, (2 * REQS,), TXT_LIVE // 4, TXT_LIVE + 1)
    chosen = jax.random.randint(pick_key, (), 0, 2 * REQS)
    other = (chosen + 1) % (2 * REQS)
    pair_ids = jnp.arange(2 * REQS, dtype=jnp.int32)
    lengths = jnp.where(pair_ids == chosen, TXT_LIVE, lengths)
    lengths = jnp.where(pair_ids == other, TXT_LIVE // 4, lengths)
    return lengths.reshape(2, REQS).astype(jnp.int32)


def draw_head_slot(key, part):
    own_key = jax.random.fold_in(key, 11)
    order_key, shard_key = jax.random.split(own_key)
    head_order = jax.random.permutation(order_key, HEADS)
    shard_rank = jnp.concatenate([jax.random.permutation(shard_key, N_SEQ - 1) + 1, jnp.zeros((1,), jnp.int32)])
    base_count = HEADS // N_SEQ
    extra_count = HEADS % N_SEQ
    slot_ids = jnp.arange(SLOTS, dtype=jnp.int32)
    owner = slot_ids // HSLOT
    within = slot_ids % HSLOT
    slot_used = (within < base_count) | (shard_rank[owner] < extra_count)
    used_rank = jnp.cumsum(slot_used.astype(jnp.int32)) - 1
    rank_ids = jnp.arange(HEADS, dtype=jnp.int32)
    hit_table = slot_used[None, :] & (used_rank[None, :] == rank_ids[:, None])
    slot_of_rank = jnp.sum(jnp.where(hit_table, slot_ids[None, :], 0), axis=1)
    table = jnp.zeros((HEADS,), jnp.int32).at[head_order].set(slot_of_rank)
    return table.astype(jnp.int32)


def set_ends(drawn, rng, smallest, top_value):
    shape = drawn.shape
    place = [jax.random.randint(jax.random.fold_in(rng, axis), (), 0, shape[axis]) for axis in range(len(shape))]
    drawn = drawn.at[tuple(place)].set(smallest)
    longest = shape.index(max(shape))
    place[longest] = (place[longest] + 1) % shape[longest]
    return drawn.at[tuple(place)].set(top_value)


def shard_levels(key, dims, cuts, low, largest):
    loudness, own = 1.0, jax.random.fold_in(key, 6)
    for dim, shards_of in cuts:
        steps = jnp.exp(jax.random.uniform(jax.random.fold_in(own, dim), (shards_of,), jnp.float32, low / len(cuts), largest / len(cuts)))
        loudness = loudness * jnp.repeat(steps, dims[dim] // shards_of).reshape([-1 if axis == dim else 1 for axis in range(len(dims))])
    return loudness


def normal_values(stream_key, dims, spread, limit, cuts=(), kind=jnp.bfloat16):
    values = jax.random.normal(stream_key, dims, jnp.float32) * spread
    if len(cuts) > 0:
        values = shard_levels(stream_key, dims, cuts, -0.22, 0.18) * values
    return jnp.clip(values, min=-limit, max=limit).astype(kind)


def setup_inputs(seed: int = 0) -> dict:
    streams_of = jax.random.split(jax.random.key(seed), 18)
    return {
        "latent": normal_values(streams_of[0], (REQS, IMG, C_OUT), 1.0, 6.0, ((0, 4), (1, 16)), jnp.float32),
        "hidden_in": draw_hidden_in(jax.random.fold_in(streams_of[17], 71), 0),
        "img_query": draw_img_query(jax.random.fold_in(streams_of[17], 71), 0),
        "img_key": draw_img_key(jax.random.fold_in(streams_of[17], 71), 0),
        "img_value": normal_values(streams_of[4], (2, REQS, IMG, D), 1.0, 6.0, ((0, 2), (1, 4), (2, 16))),
        "txt_key": draw_txt_key(jax.random.fold_in(streams_of[17], 71), 0),
        "txt_value": normal_values(streams_of[6], (2, REQS, TXT, D), 1.0, 6.0, ((0, 2), (1, 4), (2, 16))),
        "text_len": draw_text_len(jax.random.fold_in(streams_of[17], 71), 0),
        "head_slot": draw_head_slot(jax.random.fold_in(streams_of[17], 71), 0),
        "out_weight": normal_values(streams_of[9], (D, D), D ** -0.5, 0.125),
        "out_bias": normal_values(streams_of[10], (D,), 0.5, 3.0, (), jnp.float32),
        "attn_gate": jnp.clip(jnp.exp(math.log(2.0) - 1.3862944 * jax.random.uniform(streams_of[11], (2, REQS, D), jnp.float32) ** shard_levels(streams_of[11], (2, REQS, D), ((0, 2), (1, 4)), -0.2, 0.2)), 0.5, 2.0),
        "final_mod": normal_values(streams_of[12], (2, REQS, 2, D), 0.5, 3.0, ((0, 2), (1, 4)), jnp.float32),
        "final_weight": normal_values(streams_of[13], (D, C_OUT), D ** -0.5, 0.125),
        "final_bias": normal_values(streams_of[14], (C_OUT,), 0.5, 3.0, (), jnp.float32),
        "timesteps": set_ends(jax.random.randint(streams_of[15], (REQS,), 1, STEPS + 1), jax.random.fold_in(streams_of[15], 1), 1, STEPS).astype(jnp.int32),
        "guidance": jnp.clip(2.5 + 3.5 * jax.random.uniform(streams_of[16], (REQS,), jnp.float32) ** shard_levels(streams_of[16], (REQS,), ((0, 4),), -0.2, 0.2), 2.5, 6.0),
    }


masked_score = -1e+30

def sigma_of(step_idx):
    fraction = step_idx.astype(jnp.float32) / STEPS
    return 3.0 * fraction / (1.0 + 2.0 * fraction)

def attend_head(query_head, key_head, value_head, key_valid):
    scores = jnp.einsum('qd,kd->qk', query_head, key_head, preferred_element_type=jnp.float32) * (1.0 / math.sqrt(HD))
    scores = jnp.where(key_valid[None, :], scores, masked_score)
    row_top = lax.optimization_barrier(jnp.max(scores, axis=1, keepdims=True))
    weights = jnp.exp(scores - row_top)
    weights = (weights / lax.optimization_barrier(jnp.sum(weights, axis=1, keepdims=True))).astype(jnp.bfloat16)
    head_out = jnp.dot(weights, value_head, preferred_element_type=jnp.float32).astype(jnp.bfloat16)
    return (head_out, jnp.max(row_top))

def reference(latent, hidden_in, img_query, img_key, img_value, txt_key, txt_value, text_len, head_slot, out_weight, out_bias, attn_gate, final_mod, final_weight, final_bias, timesteps, guidance):

    def half_request(packed):
        hidden_row, query, key_img, value_img, key_txt, value_txt, length, gate, modul = packed
        query_heads = query.reshape(IMG, HEADS, HD).transpose(1, 0, 2)
        all_keys = jnp.concatenate([key_img, key_txt], axis=0).reshape(IMG + TXT, HEADS, HD).transpose(1, 0, 2)
        all_values = jnp.concatenate([value_img, value_txt], axis=0).reshape(IMG + TXT, HEADS, HD).transpose(1, 0, 2)
        key_valid = jnp.arange(IMG + TXT, dtype=jnp.int32) < IMG + length

        def one_head(parts):
            return attend_head(parts[0], parts[1], parts[2], key_valid)
        head_out, top_scores = lax.map(one_head, (query_heads, all_keys, all_values))
        attended = head_out.transpose(1, 0, 2).reshape(IMG, D)
        projected = jnp.dot(attended, out_weight, preferred_element_type=jnp.float32) + out_bias
        hidden = hidden_row.astype(jnp.float32) + gate[None, :] * projected
        norm_value = jnp.sqrt(jnp.mean(hidden * hidden))
        row_mean = lax.optimization_barrier(jnp.mean(hidden, axis=1, keepdims=True))
        centered = hidden - row_mean
        row_var = lax.optimization_barrier(jnp.mean(centered * centered, axis=1, keepdims=True))
        normed = (centered / jnp.sqrt(row_var + 1e-06) * (1.0 + modul[1][None, :]) + modul[0][None, :]).astype(jnp.bfloat16)
        prediction = jnp.dot(normed, final_weight, preferred_element_type=jnp.float32) + final_bias
        return (prediction, norm_value, top_scores)

    def flatten_pair(tensor):
        return tensor.reshape((2 * REQS,) + tensor.shape[2:])
    prediction, norm_values, top_scores = lax.map(half_request, (flatten_pair(hidden_in), flatten_pair(img_query), flatten_pair(img_key), flatten_pair(img_value), flatten_pair(txt_key), flatten_pair(txt_value), text_len.reshape(2 * REQS), flatten_pair(attn_gate), flatten_pair(final_mod)))
    prediction = prediction.reshape(2, REQS, IMG, C_OUT)
    scale_g = guidance[:, None, None]
    velocity = scale_g * prediction[0] + (1.0 - scale_g) * prediction[1]
    step_size = (sigma_of(timesteps - 1) - sigma_of(timesteps))[:, None, None]
    latent_next = latent + step_size * velocity
    head_peak = lax.optimization_barrier(jnp.max(top_scores, axis=0))
    max_logits = jnp.zeros((SLOTS,), jnp.float32).at[head_slot].set(head_peak)
    return (velocity, latent_next, norm_values.reshape(2, REQS), max_logits)
```

```python
import functools
import math

import jax
import jax.numpy as jnp
from jax import lax
from jax.experimental import pallas as pl
from jax.experimental.pallas import tpu as pltpu
from jax.sharding import PartitionSpec as P

STEPS = 28
HEADS = 38
HD = 64
D = 2432
TOK = 128
TXTL = 10
KROWS = 144
NS = 16
GRP = 8
QBLK = 256
LOG2_SCALE = math.log2(math.e) / math.sqrt(HD)
DEAD = -1e30
PAIR_K = TOK
PAIR_V = TOK + KROWS
PAIR_ROWS = TOK + 2 * KROWS
ONE_Q = PAIR_ROWS + KROWS
ONE_ROWS = KROWS + TOK // 2


def sigma_of(step_idx):
    fraction = step_idx.astype(jnp.float32) / STEPS
    return 3.0 * fraction / (1.0 + 2.0 * fraction)


def in_vmem(x):
    return pltpu.with_memory_space_constraint(x, pltpu.VMEM)


def low_lanes(shape):
    return lax.broadcasted_iota(jnp.int32, shape, len(shape) - 1) < HD


def swap_halves(x):
    return jnp.concatenate([x[..., HD:], x[..., :HD]], axis=-1)


def pack_kernel(q_ref, k_ref, v_ref, tk_ref, tv_ref, out_ref, *, base, with_single):
    pad = jnp.zeros((KROWS - TOK - TXTL, 128), jnp.bfloat16)

    def rows_of(img, txt, col):
        return img[0, :, col : col + 128], jnp.concatenate([txt[0, :, col : col + 128], pad], axis=0)

    for d in range(GRP):
        col = base + 128 * d
        out_ref[d, 0:TOK, :] = q_ref[0, :, col : col + 128]
        for row, img, txt in ((PAIR_K, k_ref, tk_ref), (PAIR_V, v_ref, tv_ref)):
            top, tail = rows_of(img, txt, col)
            out_ref[d, row : row + TOK, :] = top
            out_ref[d, row + TOK : row + KROWS, :] = tail
        if with_single:
            single = HEADS - 32
            if d >= single:
                out_ref[d, PAIR_ROWS:, :] = jnp.zeros((ONE_ROWS, 128), jnp.bfloat16)
                continue
            col = 2048 + 128 * (d // 2)
            k_top, k_tail = rows_of(k_ref, tk_ref, col)
            v_top, v_tail = rows_of(v_ref, tv_ref, col)
            q = q_ref[0, :, col : col + 128]

            def side(x, y):
                if d % 2 == 0:
                    return jnp.concatenate([x[:, :HD], y[:, :HD]], axis=1)
                return jnp.concatenate([x[:, HD:], y[:, HD:]], axis=1)

            out_ref[d, PAIR_ROWS : PAIR_ROWS + TOK, :] = side(k_top, v_top)
            out_ref[d, PAIR_ROWS + TOK : ONE_Q, :] = side(k_tail, v_tail)
            out_ref[d, ONE_Q:, :] = side(q[: TOK // 2], q[TOK // 2 :])


def pack(q, k, v, tk, tv, base, with_single):
    rows = PAIR_ROWS + (ONE_ROWS if with_single else 0)
    img = pl.BlockSpec((1, TOK, D), lambda r: (r, 0, 0))
    txt = pl.BlockSpec((1, TXTL, D), lambda r: (r, 0, 0))
    return pl.pallas_call(
        functools.partial(pack_kernel, base=base, with_single=with_single),
        out_shape=jax.ShapeDtypeStruct((NS, rows, 128), jnp.bfloat16),
        grid=(2,),
        in_specs=[img, img, img, txt, txt],
        out_specs=pl.BlockSpec((GRP, rows, 128), lambda r: (r, 0, 0)),
        name="pack_a" if with_single else "pack_b",
    )(q, k, v, tk, tv)


def attend_kernel(len_ref, recv_ref, out_ref, top_ref, kaug, vaug, qaug, s0, s1, p0, p1):
    head = pl.program_id(0)
    own_len = len_ref[0]
    low = low_lanes((1, 128))
    keys = NS * KROWS
    src_blk = QBLK // TOK
    blocks = NS * TOK // QBLK

    src = lax.broadcasted_iota(jnp.int32, (NS, KROWS, 128), 0)
    row = lax.broadcasted_iota(jnp.int32, (NS, KROWS, 128), 1)
    dead = (row >= TOK) & ((row >= TOK + TXTL) | (src * TXTL + row - TOK >= own_len))
    bias = jnp.where(dead, DEAD, 0.0).astype(jnp.bfloat16).reshape(keys, 128)

    def fill(own, own_v, k, v, q):
        one = jnp.ones((), jnp.bfloat16)
        zero = jnp.zeros((), jnp.bfloat16)
        kaug[:, 0:128] = jnp.where(own, k, bias)
        kaug[:, 128:256] = k
        vaug[...] = jnp.where(own_v, v, one)
        scaled = q.astype(jnp.float32) * LOG2_SCALE
        high = scaled.astype(jnp.bfloat16)
        rest = (scaled - high.astype(jnp.float32)).astype(jnp.bfloat16)
        qaug[:, 0:128] = jnp.where(own, high, one)
        qaug[:, 128:256] = jnp.where(own, rest, zero)

    def pair_parts():
        k = recv_ref[:, PAIR_K : PAIR_K + KROWS, :].reshape(keys, 128)
        v = recv_ref[:, PAIR_V : PAIR_V + KROWS, :].reshape(keys, 128)
        q = recv_ref[:, 0:TOK, :].reshape(NS * TOK, 128)
        return k, v, q

    @pl.when(head == 0)
    def _():
        fill(low, low, *pair_parts())

    @pl.when(head == 1)
    def _():
        fill(~low, ~low, *pair_parts())

    if recv_ref.shape[1] > PAIR_ROWS:

        @pl.when(head == 2)
        def _():
            kv = recv_ref[:, PAIR_ROWS:ONE_Q, :].reshape(keys, 128)
            folded = recv_ref[:, ONE_Q:, :]
            q = jnp.concatenate([folded, swap_halves(folded)], axis=1)
            fill(low, ~low, kv, kv, q.reshape(NS * TOK, 128))

    def scores(b, s_ref):
        q = qaug[b * QBLK : (b + 1) * QBLK, :]
        top = None
        for j in range(keys // 256):
            s = lax.dot_general(
                q, kaug[256 * j : 256 * (j + 1), :], (((1,), (1,)), ((), ())), preferred_element_type=jnp.float32
            )
            s_ref[:, 256 * j : 256 * (j + 1)] = s
            part = jnp.maximum(s[:, :128], s[:, 128:])
            top = part if top is None else jnp.maximum(top, part)
        return jnp.max(top, axis=1, keepdims=True)

    def finish(b, s_ref, p_ref, top):
        for j in range(keys // 256):
            cols = slice(256 * j, 256 * (j + 1))
            p_ref[:, cols] = jnp.exp2(s_ref[:, cols] - top).astype(jnp.bfloat16)
        acc = jnp.dot(p_ref[...], vaug[...], preferred_element_type=jnp.float32)
        result = (acc / swap_halves(acc)).astype(jnp.bfloat16).reshape(src_blk, TOK, 128)
        src0 = b * src_blk

        @pl.when(head == 0)
        def _():
            out_ref[src0 : src0 + src_blk, 0:TOK, 0:HD] = result[:, :, 0:HD]

        @pl.when(head == 1)
        def _():
            out_ref[src0 : src0 + src_blk, 0:TOK, HD:128] = result[:, :, HD:128]

        if recv_ref.shape[1] > PAIR_ROWS:

            @pl.when(head == 2)
            def _():
                half = TOK // 2
                first = swap_halves(result[:, :half])
                out_ref[src0 : src0 + src_blk, TOK:, :] = jnp.where(low[None], first, result[:, half:])

    tops = [scores(0, s0)]
    for b in range(blocks):
        if b + 1 < blocks:
            tops.append(scores(b + 1, (s0, s1)[(b + 1) % 2]))
        finish(b, (s0, s1)[b % 2], (p0, p1)[b % 2], tops[b])
    best = tops[0]
    for t in tops[1:]:
        best = jnp.maximum(best, t)
    best = jnp.max(best, axis=0, keepdims=True) * math.log(2.0)
    top_ref[0] = jnp.broadcast_to(best, (8, 128))


def attend(length, recv, name):
    single = recv.shape[1] > PAIR_ROWS
    heads = 3 if single else 2
    out_rows = TOK + (TOK // 2 if single else 0)
    keys = NS * KROWS
    return pl.pallas_call(
        attend_kernel,
        out_shape=(
            jax.ShapeDtypeStruct((NS, out_rows, 128), jnp.bfloat16),
            jax.ShapeDtypeStruct((heads, 8, 128), jnp.float32),
        ),
        grid_spec=pltpu.PrefetchScalarGridSpec(
            num_scalar_prefetch=1,
            grid=(heads,),
            in_specs=[pl.BlockSpec(memory_space=pltpu.VMEM)],
            out_specs=[
                pl.BlockSpec((NS, out_rows, 128), lambda h, n: (0, 0, 0)),
                pl.BlockSpec((1, 8, 128), lambda h, n: (h, 0, 0)),
            ],
            scratch_shapes=[
                pltpu.VMEM((keys, 256), jnp.bfloat16),
                pltpu.VMEM((keys, 128), jnp.bfloat16),
                pltpu.VMEM((NS * TOK, 256), jnp.bfloat16),
                pltpu.VMEM((QBLK, keys), jnp.float32),
                pltpu.VMEM((QBLK, keys), jnp.float32),
                pltpu.VMEM((QBLK, keys), jnp.bfloat16),
                pltpu.VMEM((QBLK, keys), jnp.bfloat16),
            ],
        ),
        compiler_params=pltpu.CompilerParams(vmem_limit_bytes=24 << 20),
        name=name,
    )(length, in_vmem(recv))


def project_a_kernel(recv_ref, w_pair, w0, w1, w2, bias_ref, acc_ref, x_pair, x_single):
    low = low_lanes((1, 128))
    half = TOK // 2
    for r in range(2):
        rows = slice(r * TOK, (r + 1) * TOK)
        for d in range(GRP):
            x_pair[rows, 128 * d : 128 * (d + 1)] = recv_ref[r * GRP + d, 0:TOK, :]
        for i in range(3):
            even = recv_ref[r * GRP + 2 * i, TOK:, :]
            odd = recv_ref[r * GRP + 2 * i + 1, TOK:, :]
            cols = slice(128 * i, 128 * (i + 1))
            x_single[r * TOK : r * TOK + half, cols] = jnp.where(low, even, swap_halves(odd))
            x_single[r * TOK + half : (r + 1) * TOK, cols] = jnp.where(low, swap_halves(even), odd)
    w_single = jnp.concatenate([w0[...], w1[...], w2[...]], axis=0)
    acc_ref[...] = (
        jnp.dot(x_pair[...], w_pair[...], preferred_element_type=jnp.float32)
        + jnp.dot(x_single[...], w_single, preferred_element_type=jnp.float32)
        + bias_ref[...]
    )


def whole(x):
    return pl.BlockSpec(x.shape, lambda i: (0,) * x.ndim)


def project_a(recv, weight, bias):
    singles = [pl.BlockSpec((128, D), lambda i, n=n: (n, 0)) for n in (16, 17, 18)]
    return pl.pallas_call(
        project_a_kernel,
        out_shape=jax.ShapeDtypeStruct((2 * TOK, D), jnp.float32),
        grid=(1,),
        in_specs=[whole(recv), pl.BlockSpec((1024, D), lambda i: (0, 0))] + singles + [whole(bias)],
        out_specs=pl.BlockSpec((2 * TOK, D), lambda i: (0, 0)),
        scratch_shapes=[pltpu.VMEM((2 * TOK, 1024), jnp.bfloat16), pltpu.VMEM((2 * TOK, 384), jnp.bfloat16)],
        compiler_params=pltpu.CompilerParams(vmem_limit_bytes=32 << 20),
        name="project_a",
    )(recv, weight, weight, weight, weight, bias)


def hidden_kernel(acc_ref, recv_ref, w_ref, hid_ref, gate_ref, hidden_ref, sum_ref, x):
    for r in range(2):
        for d in range(GRP):
            x[r * TOK : (r + 1) * TOK, 128 * d : 128 * (d + 1)] = recv_ref[r * GRP + d]
    projected = acc_ref[...] + jnp.dot(x[...], w_ref[...], preferred_element_type=jnp.float32)
    for r in range(2):
        hidden = hid_ref[r].astype(jnp.float32) + gate_ref[r : r + 1, :] * projected[r * TOK : (r + 1) * TOK]
        hidden_ref[r] = hidden
        square = jnp.sum(jnp.sum(hidden * hidden, axis=0, keepdims=True), axis=1, keepdims=True)
        sum_ref[r : r + 1, :] = jnp.broadcast_to(square, (1, 128))


def hidden_of(acc, recv, weight, hid, gate):
    return pl.pallas_call(
        hidden_kernel,
        out_shape=(jax.ShapeDtypeStruct((2, TOK, D), jnp.float32), jax.ShapeDtypeStruct((2, 128), jnp.float32)),
        grid=(1,),
        in_specs=[
            whole(acc),
            pl.BlockSpec(memory_space=pltpu.VMEM),
            pl.BlockSpec((1024, D), lambda i: (1, 0)),
            whole(hid),
            whole(gate),
        ],
        out_specs=[pl.BlockSpec((2, TOK, D), lambda i: (0, 0, 0)), pl.BlockSpec((2, 128), lambda i: (0, 0))],
        scratch_shapes=[pltpu.VMEM((2 * TOK, 1024), jnp.bfloat16)],
        compiler_params=pltpu.CompilerParams(vmem_limit_bytes=32 << 20),
        name="hidden",
    )(acc, in_vmem(recv), weight, hid, gate)


def predict_kernel(scale_ref, hidden_ref, mod_ref, fw_ref, fb_ref, pred_ref):
    for r in range(2):
        hidden = hidden_ref[r]
        row_mean = jnp.sum(hidden, axis=1, keepdims=True) * (1.0 / D)
        centered = hidden - row_mean
        row_var = jnp.sum(centered * centered, axis=1, keepdims=True) * (1.0 / D)
        inverse = 1.0 / jnp.sqrt(row_var + 1e-06)
        normed = centered * inverse * (1.0 + mod_ref[r, 1:2, :]) + mod_ref[r, 0:1, :]
        prediction = lax.dot_general(
            fw_ref[...], normed.astype(jnp.bfloat16), (((1,), (1,)), ((), ())), preferred_element_type=jnp.float32
        )
        pred_ref[r] = scale_ref[r] * (prediction + fb_ref[...])


def predict(scale, hidden, mod, fw, fb):
    vmem = pl.BlockSpec(memory_space=pltpu.VMEM)
    return pl.pallas_call(
        predict_kernel,
        out_shape=jax.ShapeDtypeStruct((2, 64, TOK), jnp.float32),
        in_specs=[pl.BlockSpec(memory_space=pltpu.SMEM)] + [vmem] * 4,
        compiler_params=pltpu.CompilerParams(vmem_limit_bytes=32 << 20),
        name="predict",
    )(scale, hidden, mod, fw, fb)


def gather_kernel(first_ref, shared_ref, slots_ref, norm_ref, top_ref):
    shared = shared_ref[:, 0, :]
    total = jnp.sum(shared, axis=0, keepdims=True) * (1.0 / (NS * TOK * D))
    norm_ref[...] = jnp.sqrt(total[:, 0:2])
    slots = slots_ref[...]
    lane = lax.broadcasted_iota(jnp.int32, (1, 128), 1)
    tops = jnp.zeros((1, 128), jnp.float32)
    for j in range(3):
        hit = slots == first_ref[0] + j
        best = jnp.max(jnp.max(jnp.where(hit, shared, -jnp.inf), axis=0, keepdims=True), axis=1, keepdims=True)
        tops = jnp.where((lane == j) & (best > -jnp.inf), best, tops)
    top_ref[...] = tops[:, 0:3]


def gather_small(first, shared, slots):
    vmem = pl.BlockSpec(memory_space=pltpu.VMEM)
    return pl.pallas_call(
        gather_kernel,
        out_shape=(jax.ShapeDtypeStruct((1, 2), jnp.float32), jax.ShapeDtypeStruct((1, 3), jnp.float32)),
        in_specs=[pl.BlockSpec(memory_space=pltpu.SMEM), vmem, vmem],
        name="gather_small",
    )(first, shared, slots)


def exchange(x):
    return lax.all_to_all(x, "seq", split_axis=0, concat_axis=0, tiled=True)


def local(
    latent,
    hidden_in,
    img_query,
    img_key,
    img_value,
    txt_key,
    txt_value,
    text_len,
    head_slot,
    out_weight,
    out_bias,
    attn_gate,
    final_mod,
    final_weight,
    final_bias,
    timesteps,
    guidance,
):
    position = lax.axis_index("seq")
    streams = (img_query[0], img_key[0], img_value[0], txt_key[0], txt_value[0])
    own_len = jnp.where(position < GRP, text_len[0, 0], text_len[0, 1])[None]

    send_a = pack(*streams, 0, True)
    recv_a = exchange(send_a)
    send_b = pack(*streams, 1024, False)
    recv_b = exchange(send_b)
    out_a, top_a = attend(own_len, recv_a, "attend_a")
    back_a = exchange(out_a)
    out_b, top_b = attend(own_len, recv_b, "attend_b")
    back_b = exchange(out_b)

    tops = jnp.concatenate([top_a, top_b], axis=0)[:, 0, 0]
    tops = jnp.maximum(tops, lax.ppermute(tops, "cfg", [(0, 1), (1, 0)]))
    tops = jnp.maximum(tops, lax.ppermute(tops, "req", [(i, i ^ 1) for i in range(4)]))
    tops = jnp.maximum(tops, lax.ppermute(tops, "req", [(i, i ^ 2) for i in range(4)]))

    acc = project_a(back_a, out_weight, out_bias[None])
    half_weight = jnp.where(lax.axis_index("cfg") == 0, guidance, 1.0 - guidance)
    hidden, squares = hidden_of(acc, back_b, out_weight, hidden_in[0], attn_gate[0])
    small = jnp.concatenate([squares[:, 0], tops, jnp.zeros((121,), jnp.float32)])
    shared = exchange(jnp.broadcast_to(small, (NS, 8, 128)))
    weighted = predict(half_weight, hidden, final_mod[0], final_weight.T, final_bias[:, None])
    single_slots = jnp.concatenate([head_slot[32:], jnp.full((2,), -1, jnp.int32)])
    slots = jnp.concatenate(
        [head_slot[:16].reshape(GRP, 2), single_slots[:, None], head_slot[16:32].reshape(GRP, 2)], axis=1
    )
    slots = jnp.pad(jnp.concatenate([slots, slots], axis=0), ((0, 0), (2, 121)), constant_values=-1)
    hidden_norms, own_top = gather_small((position * 3)[None], shared, slots)
    max_logits = own_top.reshape(3)

    velocity = weighted + lax.ppermute(weighted, "cfg", [(0, 1), (1, 0)])
    step_size = (sigma_of(timesteps - 1) - sigma_of(timesteps))[:, None, None]
    latent_next = latent.transpose(0, 2, 1) + step_size * velocity
    return (velocity.transpose(0, 2, 1), latent_next.transpose(0, 2, 1), hidden_norms, max_logits)


def solution(mesh):
    in_specs = (
        P("req", "seq", None),
        P("cfg", "req", "seq", None),
        P("cfg", "req", "seq", None),
        P("cfg", "req", "seq", None),
        P("cfg", "req", "seq", None),
        P("cfg", "req", "seq", None),
        P("cfg", "req", "seq", None),
        P("cfg", "req"),
        P(),
        P(),
        P(),
        P("cfg", "req", None),
        P("cfg", "req", None, None),
        P(),
        P(),
        P("req"),
        P("req"),
    )
    out_specs = (P("req", "seq", None), P("req", "seq", None), P("cfg", "req"), P("seq"))
    return jax.shard_map(local, mesh=mesh, in_specs=in_specs, out_specs=out_specs, check_vma=False)
```
